32 devices in a mesh: groups: 2 (over y), tensor: 4 (over z), dp: 4 (over x, core).
Axes of the slice: x: 2, y: 2, z: 4, core: 2. Of those that a mesh axis runs over, the one named last changes fastest.
Arguments:
- root_features: bfloat16 [32, 16384], P('groups', 'dp'), parts along dimension 0, may hold values from -6 to 6
- branch_embeds: bfloat16 [32, 4, 8, 16384], P('groups', None, None, 'dp'), parts along dimension 0, may hold values from -6 to 6
- parents: int32 [32, 3, 8], P('groups'), parts along dimension 0, may hold values from 0 to 7
- cache_lengths: int32 [32], P(('groups', 'dp')), parts along dimension 0, may hold values from 128 to 512, as said below
- cache_kv: bfloat16 [32, 2, 512, 512], P(('groups', 'dp'), None, None, 'tensor'), parts along dimension 0, may hold values from -6 to 6, as said below
- norm_gain: bfloat16 [16384], P('dp'), may hold values from 0.099609375 to 1.8984375
- w_query: bfloat16 [16384, 2048], P('dp', 'tensor'), may hold values from -1 to 1
- w_keyval: bfloat16 [16384, 2, 512], P('dp', None, 'tensor'), may hold values from -1 to 1, as said below
- w_out: bfloat16 [2048, 16384], P('tensor', 'dp'), may hold values from -0.125 to 0.125
Outputs:
- tree_features: bfloat16 [32, 4, 8, 16384], P('groups', None, None, ('dp', 'tensor')), parts along dimension 0
The draws below stay inside these ranges and needn't reach their ends.
There are 2 independent parts, one for each index of `groups`. The reference program is written for one: setup_inputs(seed, part) draws one part's arguments, and reference() takes and returns one part's arrays. A program takes and returns all parts, laid end to end along the dimension named above; an argument that names none is the same for every part. Nothing has to cross between parts.
Inputs may be any that keep to these rules, and one draw needn't show every extreme that they name: `cache_lengths`: some request has exactly 512 valid cache positions and some other exactly 128. `cache_kv`: for each request, keys and values, the 4 blocks of 128 columns k * 4 .. (k + 1) * 4 - 1 are equal; they hold key-value head k. `w_keyval`: for keys and values, the 4 blocks of 128 columns k * 4 .. (k + 1) * 4 - 1 are equal; they hold key-value head k.
All inputs are finite; a program needn't handle non-finite values.
Results may differ from the reference program's by a relative error of at most 0.017.
Values may be sent and summed in bfloat16 or wider, within the bound.
A program may use at most 128 MiB of HBM per device.

```python
import jax
import jax.numpy as jnp
from jax import lax

D = 16384
HD = 128
HEADS_DEV = 4
BRANCH = 8
DEPTHS = 4
CACHE = 512
REQUESTS = 16
HEADS = 16
KV = 1
COPIES = 4
N_TENSOR = 4


def draw_cache_lengths(key, part):
    first, second, third = jax.random.split(jax.random.fold_in(key, 17), 3)
    lengths = jax.random.randint(first, (REQUESTS,), CACHE // 4, CACHE + 1, dtype=jnp.int32)
    longest = jax.random.randint(second, (), 0, REQUESTS, dtype=jnp.int32)
    offset = jax.random.randint(third, (), 1, REQUESTS, dtype=jnp.int32)
    shortest = (longest + offset) % REQUESTS
    index_row = jnp.arange(REQUESTS, dtype=jnp.int32)
    lengths = jnp.where(index_row == shortest, CACHE // 4, lengths)
    return jnp.where(index_row == longest, CACHE, lengths).astype(jnp.int32)


def draw_cache_kv(key, part):
    entries = jax.random.normal(jax.random.fold_in(key, 37), (REQUESTS, 2, CACHE, KV, 1, HD), jnp.float32)
    entries = jnp.clip(entries, -6.0, 6.0)
    copied = jnp.broadcast_to(entries, (REQUESTS, 2, CACHE, KV, COPIES, HD))
    return copied.reshape(REQUESTS, 2, CACHE, KV * COPIES * HD).astype(jnp.bfloat16)


def shared_blocks(key):
    key_seed, value_seed = jax.random.split(jax.random.fold_in(key, 29), 2)
    key_block = jnp.clip(jax.random.normal(key_seed, (D, KV, HD), jnp.float32), -6.0, 6.0)
    value_block = jnp.clip(jax.random.normal(value_seed, (D, KV, HD), jnp.float32), -6.0, 6.0)
    return (key_block, value_block)


def draw_w_keyval(key, part):
    key_block, value_block = shared_blocks(key)
    stacked = jnp.stack([key_block, value_block], axis=1) * D ** (-0.5)
    copied = jnp.broadcast_to(stacked[:, :, :, None, :], (D, 2, KV, COPIES, HD))
    return jnp.clip(copied, -1.0, 1.0).reshape(D, 2, KV * COPIES * HD).astype(jnp.bfloat16)


def draw_w_query(key, part):
    base_seed = jax.random.fold_in(jax.random.fold_in(key, 31), 0)
    total = jnp.clip(jax.random.normal(base_seed, (D, HEADS, HD), jnp.float32), -6.0, 6.0)
    return jnp.clip(total * D ** (-0.5), -1.0, 1.0).reshape(D, HEADS * HD).astype(jnp.bfloat16)


def touch_ends(values, key, smallest, top_value):
    spot = [jax.random.randint(jax.random.fold_in(key, axis), (), 0, length) for axis, length in enumerate(values.shape)]
    widest = values.shape.index(max(values.shape))
    neighbour = spot[:widest] + [(spot[widest] + 1) % values.shape[widest]] + spot[widest + 1:]
    return values.at[tuple(spot)].set(smallest).at[tuple(neighbour)].set(top_value)


def levels(key, shape, pieces, smallest, high):
    def one(position, shards_of):
        steps = jax.random.uniform(jax.random.fold_in(jax.random.fold_in(key, 6), position), (shards_of,), jnp.float32, smallest / len(pieces), high / len(pieces))
        return jnp.repeat(jnp.exp(steps), shape[position] // shards_of).reshape((-1,) + (1,) * (len(shape) - position - 1))

    level = one(*pieces[0])
    for cut in pieces[1:]:
        level = level * one(*cut)
    return level


def gaussian(own_key, extent, spread, reach, pieces=(), held_as=jnp.bfloat16):
    factor_of = levels(own_key, extent, pieces, -0.22, 0.18) if pieces else 1.0
    array = jax.random.normal(own_key, extent, jnp.float32) * spread * factor_of
    return jnp.minimum(jnp.maximum(array, -reach), reach).astype(held_as)


def setup_inputs(seed: int = 0, part: int = 0) -> dict:
    arg_keys = jax.random.split(jax.random.key(seed), 10)
    part_keys = jax.random.split(jax.random.fold_in(arg_keys[9], part), 10)
    return {
        "root_features": gaussian(part_keys[0], (REQUESTS, D), 1.0, 6.0, ((1, 4),)),
        "branch_embeds": gaussian(part_keys[1], (REQUESTS, DEPTHS, BRANCH, D), 1.0, 6.0, ((3, 4),)),
        "parents": touch_ends(jax.random.randint(part_keys[2], (REQUESTS, DEPTHS - 1, BRANCH), 0, BRANCH), jax.random.fold_in(part_keys[2], 1), 0, BRANCH - 1).astype(jnp.int32),
        "cache_lengths": draw_cache_lengths(jax.random.fold_in(jax.random.fold_in(arg_keys[9], part), 71), part),
        "cache_kv": draw_cache_kv(jax.random.fold_in(jax.random.fold_in(arg_keys[9], part), 71), part),
        "norm_gain": jnp.clip(1.0 + 0.18 * jax.random.normal(arg_keys[5], (D,), jnp.float32), 0.099609375, 1.8984375).astype(jnp.bfloat16),
        "w_query": draw_w_query(jax.random.fold_in(arg_keys[9], 71), part),
        "w_keyval": draw_w_keyval(jax.random.fold_in(arg_keys[9], 71), part),
        "w_out": gaussian(arg_keys[8], (HEADS * HD, D), (HEADS * HD) ** -0.5, 0.125, ((0, 4), (1, 4))),
    }


epsilon = 1e-05
masked_score = -1e+30

def ancestor_path(parent_table, tree_level):
    current = jnp.broadcast_to(jnp.arange(BRANCH, dtype=jnp.int32)[None, :], (parent_table.shape[0], BRANCH))
    path_nodes = [current]
    for upper in range(tree_level, 0, -1):
        current = jnp.take_along_axis(parent_table[:, upper - 1], current, axis=1)
        path_nodes.append(current)
    return path_nodes[::-1]

def tree_mask_of(parent_table, tree_level):
    path_nodes = ancestor_path(parent_table, tree_level)
    columns = jnp.arange(BRANCH, dtype=jnp.int32)
    blocks = []
    for other_level in range(DEPTHS):
        if other_level <= tree_level:
            blocks.append(columns[None, None, :] == path_nodes[other_level][:, :, None])
        else:
            blocks.append(jnp.zeros((parent_table.shape[0], BRANCH, BRANCH), dtype=bool))
    return jnp.concatenate(blocks, axis=2)

def attend_one(packed):
    queries, cache_keys, cache_values, tree_keys, tree_values, cache_valid, tree_mask = packed
    kv_heads = cache_keys.shape[1]
    grouped = queries.astype(jnp.float32).reshape(BRANCH, kv_heads, -1, HD)
    cache_scores = jnp.einsum('bkgd,ckd->kgbc', grouped, cache_keys.astype(jnp.float32)) * HD ** (-0.5)
    tree_scores = jnp.einsum('bkgd,tkd->kgbt', grouped, tree_keys.astype(jnp.float32)) * HD ** (-0.5)
    cache_scores = jnp.where(cache_valid[None, None, None, :], cache_scores, masked_score)
    tree_scores = jnp.where(tree_mask[None, None, :, :], tree_scores, masked_score)
    row_max = jnp.maximum(lax.optimization_barrier(jnp.max(cache_scores, axis=3)), lax.optimization_barrier(jnp.max(tree_scores, axis=3)))[..., None]
    cache_exp = jnp.exp(cache_scores - row_max)
    tree_exp = jnp.exp(tree_scores - row_max)
    denominator = lax.optimization_barrier(jnp.sum(cache_exp, axis=3, keepdims=True)) + lax.optimization_barrier(jnp.sum(tree_exp, axis=3, keepdims=True))
    cache_weights = (cache_exp / denominator).astype(jnp.bfloat16)
    tree_weights = (tree_exp / denominator).astype(jnp.bfloat16)
    mixed = jnp.einsum('kgbc,ckd->bkgd', cache_weights.astype(jnp.float32), cache_values.astype(jnp.float32))
    mixed = mixed + jnp.einsum('kgbt,tkd->bkgd', tree_weights.astype(jnp.float32), tree_values.astype(jnp.float32))
    return mixed.reshape(BRANCH, -1).astype(jnp.bfloat16)

def reference(root_features, branch_embeds, parents, cache_lengths, cache_kv, norm_gain, w_query, w_keyval, w_out):
    request_count = root_features.shape[0]
    kv_heads = KV
    kv_cols = kv_heads * HD
    all_rows = request_count * BRANCH
    first_copy = cache_kv.reshape(request_count, 2, CACHE, kv_heads, COPIES, HD)[:, :, :, :, 0]
    cache_keys = first_copy[:, 0]
    cache_values = first_copy[:, 1]
    positions = jnp.arange(CACHE, dtype=jnp.int32)
    cache_valid = positions[None, :] < cache_lengths[:, None]
    tree_keys = jnp.zeros((request_count, DEPTHS * BRANCH, kv_heads, HD), jnp.bfloat16)
    tree_values = jnp.zeros((request_count, DEPTHS * BRANCH, kv_heads, HD), jnp.bfloat16)
    keyval_weight = w_keyval.reshape(D, 2, kv_heads, COPIES, HD)[:, :, :, 0].reshape(D, 2 * kv_cols)
    out_blocks = w_out.reshape(N_TENSOR, HEADS_DEV * HD, D)
    gain = norm_gain.astype(jnp.float32)
    results = []
    previous = None
    for tree_level in range(DEPTHS):
        if tree_level == 0:
            parent = jnp.broadcast_to(root_features[:, None, :], (request_count, BRANCH, D))
        else:
            parent = jnp.take_along_axis(previous, parents[:, tree_level - 1][:, :, None], axis=1)
        node_state = parent.astype(jnp.float32) + branch_embeds[:, tree_level].astype(jnp.float32)
        flat_state = node_state.reshape(all_rows, D)
        inv_rms = lax.rsqrt(lax.optimization_barrier(jnp.mean(flat_state * flat_state, axis=1, keepdims=True)) + epsilon)
        scaled = (flat_state * gain).astype(jnp.bfloat16)
        queries = (jnp.dot(scaled, w_query, preferred_element_type=jnp.float32) * inv_rms).astype(jnp.bfloat16)
        keyval = (jnp.dot(scaled, keyval_weight, preferred_element_type=jnp.float32) * inv_rms).astype(jnp.bfloat16)
        new_keys = keyval[:, :kv_cols].reshape(request_count, BRANCH, kv_heads, HD)
        new_values = keyval[:, kv_cols:].reshape(request_count, BRANCH, kv_heads, HD)
        tree_keys = tree_keys.at[:, tree_level * BRANCH:(tree_level + 1) * BRANCH].set(new_keys)
        tree_values = tree_values.at[:, tree_level * BRANCH:(tree_level + 1) * BRANCH].set(new_values)
        tree_mask = tree_mask_of(parents, tree_level)
        attended = lax.map(attend_one, (queries.reshape(request_count, BRANCH, -1), cache_keys, cache_values, tree_keys, tree_values, cache_valid, tree_mask))
        head_groups = jnp.swapaxes(attended.reshape(all_rows, N_TENSOR, HEADS_DEV * HD), 0, 1)

        def add_group(carry, pair):
            group_rows, group_weight = pair
            partial_sum = jnp.dot(group_rows, group_weight, preferred_element_type=jnp.float32).astype(jnp.bfloat16)
            partial_sum = lax.optimization_barrier(partial_sum)
            return (carry + partial_sum.astype(jnp.float32), None)
        summed, _ = lax.scan(add_group, jnp.zeros((all_rows, D), jnp.float32), (head_groups, out_blocks))
        fresh = (flat_state + summed).astype(jnp.bfloat16).reshape(request_count, BRANCH, D)
        results.append(fresh)
        previous = fresh
    return jnp.stack(results, axis=1)
```

```python
import functools

import jax
import jax.numpy as jnp
from jax import lax
from jax.experimental import pallas as pl
from jax.experimental.pallas import tpu as pltpu
from jax.sharding import PartitionSpec as P

D = 16384
HD = 128
BRANCH = 8
DEPTHS = 4
CACHE = 512
BATCHES = 2
PER = 4
HOP = 2.8
PACE = 0.65
PERIOD = 12.5
TURN = 7.2
PROJ_TRIP = 2.9
SLACK = 0.5


epsilon = 1e-05
masked_score = -1e30


def ancestor_path(parent_table, tree_level):
    current = jnp.broadcast_to(
        jnp.arange(BRANCH, dtype=jnp.int32)[None, :], (parent_table.shape[0], BRANCH)
    )
    path_nodes = [current]
    for upper in range(tree_level, 0, -1):
        current = jnp.take_along_axis(parent_table[:, upper - 1], current, axis=1)
        path_nodes.append(current)
    return path_nodes[::-1]


def tree_mask_of(parent_table, tree_level):
    path_nodes = ancestor_path(parent_table, tree_level)
    columns = jnp.arange(BRANCH, dtype=jnp.int32)
    blocks = []
    for other_level in range(DEPTHS):
        if other_level <= tree_level:
            blocks.append(columns[None, None, :] == path_nodes[other_level][:, :, None])
        else:
            blocks.append(jnp.zeros((parent_table.shape[0], BRANCH, BRANCH), dtype=bool))
    return jnp.concatenate(blocks, axis=2)


def shards(
    root_features,
    branch_embeds,
    parents,
    cache_lengths,
    cache_kv,
    norm_gain,
    w_query,
    w_keyval,
    w_out,
):
    request_count, feat_cols = root_features.shape
    local_requests = cache_lengths.shape[0]
    head_cols = w_query.shape[1]
    kv_cols = w_keyval.shape[2]
    kv_local = kv_cols // HD
    all_rows = request_count * BRANCH
    own_rows = local_requests * BRANCH
    share_cols = feat_cols // lax.axis_size("tensor")
    dp_index = lax.axis_index("dp")
    tensor_index = lax.axis_index("tensor")
    weights = jnp.concatenate([w_query, w_keyval.reshape(feat_cols, 2 * kv_cols)], axis=1)
    gain = norm_gain.astype(jnp.float32)
    own_parents = lax.dynamic_slice_in_dim(parents, dp_index * local_requests, local_requests, 0)
    cache_keys = cache_kv[:, 0].reshape(local_requests, CACHE, kv_local, HD)
    cache_values = cache_kv[:, 1].reshape(local_requests, CACHE, kv_local, HD)
    positions = jnp.arange(CACHE, dtype=jnp.int32)
    cache_valid = positions[None, :] < cache_lengths[:, None]
    tree_keys = jnp.zeros((local_requests, DEPTHS * BRANCH, kv_local, HD), jnp.bfloat16)
    tree_values = jnp.zeros((local_requests, DEPTHS * BRANCH, kv_local, HD), jnp.bfloat16)
    results = []
    previous = None
    for tree_level in range(DEPTHS):
        if tree_level == 0:
            parent = jnp.broadcast_to(root_features[:, None, :], (request_count, BRANCH, feat_cols))
        else:
            parent = jnp.take_along_axis(previous, parents[:, tree_level - 1][:, :, None], axis=1)
        node_state = parent.astype(jnp.float32) + branch_embeds[:, tree_level].astype(jnp.float32)
        flat_state = node_state.reshape(all_rows, feat_cols)
        square_sums = jnp.sum(flat_state * flat_state, axis=1)
        scaled = (flat_state * gain).astype(jnp.bfloat16)
        total_sums = lax.psum(square_sums, "dp")
        own_sums = lax.dynamic_slice_in_dim(total_sums, dp_index * own_rows, own_rows, 0)
        proj_terms = lax.psum_scatter(
            jnp.dot(scaled, weights, preferred_element_type=jnp.float32).astype(jnp.bfloat16),
            "dp",
            scatter_dimension=0,
            tiled=True,
        ).astype(jnp.float32)
        inv_rms = lax.rsqrt(own_sums / D + epsilon)[:, None]
        projected = (proj_terms * inv_rms).astype(jnp.bfloat16)
        queries = projected[:, :head_cols].reshape(local_requests, BRANCH, kv_local, -1, HD)
        new_keys = projected[:, head_cols : head_cols + kv_cols].reshape(
            local_requests, BRANCH, kv_local, HD
        )
        new_values = projected[:, head_cols + kv_cols :].reshape(
            local_requests, BRANCH, kv_local, HD
        )
        tree_keys = tree_keys.at[:, tree_level * BRANCH : (tree_level + 1) * BRANCH].set(new_keys)
        tree_values = tree_values.at[:, tree_level * BRANCH : (tree_level + 1) * BRANCH].set(
            new_values
        )
        tree_mask = tree_mask_of(own_parents, tree_level)
        cache_scores = jnp.einsum(
            "rbkgd,rckd->rkgbc", queries, cache_keys, preferred_element_type=jnp.float32
        ) * HD ** (-0.5)
        tree_scores = jnp.einsum(
            "rbkgd,rtkd->rkgbt", queries, tree_keys, preferred_element_type=jnp.float32
        ) * HD ** (-0.5)
        cache_scores = jnp.where(cache_valid[:, None, None, None, :], cache_scores, masked_score)
        tree_scores = jnp.where(tree_mask[:, None, None, :, :], tree_scores, masked_score)
        row_max = jnp.maximum(jnp.max(cache_scores, axis=4), jnp.max(tree_scores, axis=4))[
            ..., None
        ]
        cache_exp = jnp.exp(cache_scores - row_max)
        tree_exp = jnp.exp(tree_scores - row_max)
        denominator = jnp.sum(cache_exp, axis=4, keepdims=True) + jnp.sum(
            tree_exp, axis=4, keepdims=True
        )
        cache_weights = (cache_exp / denominator).astype(jnp.bfloat16)
        tree_weights = (tree_exp / denominator).astype(jnp.bfloat16)
        mixed = jnp.einsum(
            "rkgbc,rckd->rbkgd", cache_weights, cache_values, preferred_element_type=jnp.float32
        )
        mixed = mixed + jnp.einsum(
            "rkgbt,rtkd->rbkgd", tree_weights, tree_values, preferred_element_type=jnp.float32
        )
        attended = mixed.reshape(own_rows, head_cols).astype(jnp.bfloat16)
        partial_out = jnp.dot(
            lax.all_gather(attended, "dp", axis=0, tiled=True),
            w_out,
            preferred_element_type=jnp.float32,
        )
        share_sums = lax.psum_scatter(
            partial_out.astype(jnp.bfloat16), "tensor", scatter_dimension=1, tiled=True
        ).astype(jnp.float32)
        residual = lax.dynamic_slice_in_dim(flat_state, tensor_index * share_cols, share_cols, 1)
        fresh_share = (residual + share_sums).astype(jnp.bfloat16)
        if tree_level + 1 < DEPTHS:
            gathered = lax.all_gather(fresh_share, "tensor", axis=1, tiled=True)
            previous = gathered.reshape(request_count, BRANCH, feat_cols)
        results.append(fresh_share.reshape(request_count, BRANCH, share_cols))
    return jnp.stack(results, axis=1)


MESH = pl.DeviceIdType.MESH


def dot32(a, b):
    return jnp.dot(a, b, preferred_element_type=jnp.float32)


def dot32_t(a, b):
    return lax.dot_general(a, b, (((1,), (1,)), ((), ())), preferred_element_type=jnp.float32)


def timetable(n, chunks):
    per = chunks // n
    jobs = []
    for s in range(chunks):
        for hops in range(1, n - 1):
            jobs.append((HOP * hops + PACE * s, hops, s))
        if s % per == per - 1:
            jobs.append((HOP * (n - 1) + PACE * s + SLACK, n - 1, s // per))
    phases = ([], [], [])
    for time, hops, s in jobs:
        age, when = 1, time
        while when >= PERIOD:
            age, when = age + 1, when - PERIOD
        phase = 0 if when < PERIOD - TURN else 1 if when < PERIOD - TURN + PROJ_TRIP else 2
        if age > BATCHES or (age == BATCHES and phase > 0):
            age, phase, when = BATCHES, 0, when + PERIOD * (age - BATCHES)
        phases[phase].append((when, -age, hops, s))
    return [[(-age, hops, s) for _, age, hops, s in sorted(phase)] for phase in phases]


def tree_kernel(
    n,
    m,
    root_ref,
    emb_hbm,
    hot_ref,
    len_ref,
    cache_hbm,
    gain_ref,
    wq_hbm,
    wkv_hbm,
    wo_hbm,
    out_ref,
    emb,
    cache,
    wq,
    wkv,
    wo,
    scaled,
    state,
    part,
    right_send,
    right_recv,
    left_send,
    left_recv,
    proj,
    proj_send,
    proj_recv,
    squares,
    sums_recv,
    tree_keys,
    tree_values,
    tree_mask,
    att,
    load_sem,
    right_ssem,
    right_rsem,
    left_ssem,
    left_rsem,
    proj_ssem,
    proj_rsem,
    dsum_ssem,
    dsum_rsem,
    att_ssem,
    att_rsem,
):
    t = lax.axis_index("tensor")
    d = lax.axis_index("dp")
    requests, feat = root_ref.shape
    own_requests = requests // m
    part_requests = own_requests // BATCHES
    own = part_requests * BRANCH
    rows = own * m
    head_cols = wq.shape[1]
    heads = head_cols // HD
    steps = BATCHES * DEPTHS
    chunks, _, width = right_send.shape[1:]
    per = chunks // n
    tail = steps - BATCHES

    def cols_of(c, count=1):
        return slice(c * width, (c + count) * width)

    def batch_rows(b):
        return [pl.ds(k * own_requests + b * part_requests, part_requests) for k in range(m)]

    def joined(blocks, columns):
        return jnp.concatenate(blocks, axis=0).astype(jnp.float32).reshape(rows, columns)

    loads = [
        pltpu.make_async_copy(emb_hbm.at[:, 0], emb.at[0], load_sem.at[0]),
        pltpu.make_async_copy(wq_hbm, wq, load_sem.at[1]),
        pltpu.make_async_copy(wkv_hbm, wkv, load_sem.at[2]),
        pltpu.make_async_copy(cache_hbm, cache, load_sem.at[3]),
    ]
    for s in range(n):
        columns = slice(s * per * width, (s + 1) * per * width)
        loads.append(pltpu.make_async_copy(wo_hbm.at[:, columns], wo.at[s], load_sem.at[4 + s]))
    for e in range(1, DEPTHS):
        loads.append(
            pltpu.make_async_copy(emb_hbm.at[:, e], emb.at[e], load_sem.at[3 + n + e])
        )
    for load in loads:
        load.start()

    dp_to = [lax.rem(d + k, m) for k in range(1, m)]

    barrier = pltpu.get_barrier_semaphore()
    for peer in dp_to:
        pl.semaphore_signal(barrier, inc=1, device_id={"dp": peer}, device_id_type=MESH)

    for k in range(1, n):
        peer = lax.rem(t + k, n)
        pl.semaphore_signal(barrier, inc=1, device_id={"tensor": peer}, device_id_type=MESH)

    def right_copy(p, c):
        return pltpu.make_async_remote_copy(
            src_ref=right_send.at[p, c],
            dst_ref=right_recv.at[p, c],
            send_sem=right_ssem.at[p, c],
            recv_sem=right_rsem.at[p, c],
            device_id={"tensor": lax.rem(t + 1, n)},
            device_id_type=MESH,
        )

    def left_copy(p, c):
        return pltpu.make_async_remote_copy(
            src_ref=left_send.at[p, c],
            dst_ref=left_recv.at[p, c],
            send_sem=left_ssem.at[p, c],
            recv_sem=left_rsem.at[p, c],
            device_id={"tensor": lax.rem(t + n - 1, n)},
            device_id_type=MESH,
        )

    def proj_copy(i, k):
        return pltpu.make_async_remote_copy(
            src_ref=proj_send.at[i, dp_to[k]],
            dst_ref=proj_recv.at[i, k],
            send_sem=proj_ssem.at[i, k],
            recv_sem=proj_rsem.at[i, k],
            device_id={"dp": dp_to[k]},
            device_id_type=MESH,
        )

    def dsum_copy(i, k):
        return pltpu.make_async_remote_copy(
            src_ref=squares.at[i, dp_to[k]],
            dst_ref=sums_recv.at[i, k],
            send_sem=dsum_ssem.at[i, k],
            recv_sem=dsum_rsem.at[i, k],
            device_id={"dp": dp_to[k]},
            device_id_type=MESH,
        )

    def att_copy(i, k):
        return pltpu.make_async_remote_copy(
            src_ref=att.at[i, d],
            dst_ref=att.at[i, d],
            send_sem=att_ssem.at[i, k],
            recv_sem=att_rsem.at[i, k],
            device_id={"dp": dp_to[k]},
            device_id_type=MESH,
        )

    def right_limit(p):
        return jnp.where(p < tail, chunks, (n - 1 - t) * per)

    def left_limit(p):
        return jnp.where(p < tail, chunks, t * per)

    def right_chunk(p, s):
        return jnp.where(p < tail, s, chunks - 1 - s)

    def relay_right(p, s):
        @pl.when(s < right_limit(p))
        def _():
            c = right_chunk(p, s)
            right_copy(p, c).wait_recv()
            block = part[lax.rem(p, BATCHES), c] + right_recv[p, c].astype(jnp.float32)
            right_send[p, c] = block.astype(jnp.bfloat16)
            right_copy(p, c).start()

    def relay_left(p, s):
        @pl.when(s < left_limit(p))
        def _():
            left_copy(p, s).wait_recv()
            block = part[lax.rem(p, BATCHES), s] + left_recv[p, s].astype(jnp.float32)
            left_send[p, s] = block.astype(jnp.bfloat16)
            left_copy(p, s).start()

    def relays(p, hops, s):
        for place in range(1, n - 1):
            if hops not in (place, n - 1 - place):
                continue

            @pl.when((t == place) & (p >= 0))
            def _():
                if hops == place:
                    relay_right(p, s)
                if hops == n - 1 - place:
                    relay_left(p, s)

    def product(b, c, count, first):
        block = scaled[b, :, cols_of(c, count)]
        left, right = dot32(block, wq[cols_of(c, count)]), dot32(block, wkv[cols_of(c, count)])
        if first:
            proj[b, :, :head_cols] = left
            proj[b, :, head_cols:] = right
        else:
            proj[b, :, :head_cols] += left
            proj[b, :, head_cols:] += right

    def feed(i, c, node):
        b = lax.rem(i, BATCHES)
        state[b, c] = node
        gain = gain_ref[:, cols_of(c)].astype(jnp.float32)
        scaled[b, :, cols_of(c)] = (node * gain).astype(jnp.bfloat16)
        folded = jnp.zeros((rows, HD), jnp.float32)
        for low in range(0, width, HD):
            piece = node[:, low : low + HD]
            folded = folded + piece * piece
        folded = folded.reshape(m, own, HD)
        if c == 0:
            squares[i] = folded
        else:
            squares[i] += folded

    def keep(e, b, value, local):
        for k, r in enumerate(batch_rows(b)):
            out_ref[r, pl.ds(e, 1), :, local * width : (local + 1) * width] = (
                value[k * own : (k + 1) * own].reshape(part_requests, 1, BRANCH, width)
            )

    def finish(p, seg):
        b = lax.rem(p, BATCHES)
        e = p // BATCHES
        group = range(seg * per, (seg + 1) * per)

        @pl.when(t == 0)
        def _():
            for c in group:
                left_copy(p, c).wait_recv()

        @pl.when(t == n - 1)
        def _():
            for c in group:
                right_copy(p, c).wait_recv()

        whole = [
            (
                state[b, c]
                + part[b, c]
                + right_recv[p, c].astype(jnp.float32)
                + left_recv[p, c].astype(jnp.float32)
            ).astype(jnp.bfloat16)
            for c in group
        ]
        hot = hot_ref[p]
        for c, fresh in zip(group, whole):
            embeds = joined([emb[e + 1, r, :, cols_of(c)] for r in batch_rows(b)], width)
            feed(p + BATCHES, c, dot32(hot, fresh) + embeds)
        product(b, seg * per, per, seg == 0)

        @pl.when(t == seg)
        def _():
            for c, fresh in zip(group, whole):
                keep(e, b, fresh, c % per)

    def finish_last(p):
        b = lax.rem(p, BATCHES)
        e = p // BATCHES
        for local in range(per):
            c = t * per + local

            @pl.when(t > 0)
            def _():
                right_copy(p, c).wait_recv()

            @pl.when(t < n - 1)
            def _():
                left_copy(p, c).wait_recv()

            total = (
                state[b, c]
                + part[b, c]
                + right_recv[p, c].astype(jnp.float32)
                + left_recv[p, c].astype(jnp.float32)
            )
            keep(e, b, total.astype(jnp.bfloat16), local)

    row_id = lax.broadcasted_iota(jnp.int32, (rows, requests), 0)
    request_id = lax.broadcasted_iota(jnp.int32, (rows, requests), 1)

    def first_states(b):
        place = row_id // BRANCH
        request = (
            place // part_requests * own_requests + b * part_requests + place % part_requests
        )
        root_hot = (request == request_id).astype(jnp.bfloat16)
        for c in range(chunks):
            embeds = joined([emb[0, r, :, cols_of(c)] for r in batch_rows(b)], width)
            feed(b, c, dot32(root_hot, root_ref[:, cols_of(c)]) + embeds)

    def first_product(b):
        for c in range(0, chunks, per):
            product(b, c, per, c == 0)

    tree_keys[...] = jnp.zeros_like(tree_keys)
    tree_values[...] = jnp.zeros_like(tree_values)
    tree_mask[...] = jnp.zeros_like(tree_mask)

    @pl.when(t == 0)
    def _():
        right_recv[...] = jnp.zeros_like(right_recv)

    @pl.when(t == n - 1)
    def _():
        left_recv[...] = jnp.zeros_like(left_recv)

    loads[0].wait()
    first_states(0)
    loads[1].wait()
    loads[2].wait()
    first_product(0)
    pl.semaphore_wait(barrier, m + n - 2)

    timed = timetable(n, chunks)

    def run(i, phase):
        for age, hops, s in timed[phase]:
            p = i - age
            if hops < n - 1:
                relays(p, hops, s)
            else:

                @pl.when((p >= 0) & (p < tail))
                def _():
                    finish(p, s)

    def relay_rest(p):
        for age in range(max(1, steps - p), BATCHES + 1):
            for phase in range(3):
                for job_age, hops, s in timed[phase]:
                    if job_age == age and hops < n - 1:
                        relays(p, hops, s)

    def step(i, carry):
        b = lax.rem(i, BATCHES)
        e = i // BATCHES

        with jax.named_scope("A_tail"):

            run(i, 0)

        with jax.named_scope("B_send"):
            for k in range(m):
                proj_send[i, k] = proj[b, k * own : (k + 1) * own].astype(jnp.bfloat16)
            for k in range(m - 1):
                proj_copy(i, k).start()
                dsum_copy(i, k).start()

        with jax.named_scope("C_mid"):

            @pl.when(i < BATCHES - 1)
            def _():
                first_states(i + 1)
                first_product(i + 1)

            run(i, 1)
            own_row = lax.broadcasted_iota(jnp.int32, (own, DEPTHS * own), 0)
            own_col = lax.broadcasted_iota(jnp.int32, (own, DEPTHS * own), 1)
            itself = (own_col == own_row + e * own).astype(jnp.float32)
            own_rows = pl.ds(pl.multiple_of(d * own, own), own)
            mask_now = itself + dot32(hot_ref[jnp.maximum(i - BATCHES, 0), own_rows], tree_mask[b])
            tree_mask[b, own_rows] = mask_now.astype(jnp.bfloat16)

        projected = proj[b, pl.ds(pl.multiple_of(d * own, own), own)]
        summed = squares[i, d]
        with jax.named_scope("D_projwait"):
            for k in range(m - 1):
                proj_copy(i, k).wait_recv()
                dsum_copy(i, k).wait_recv()
                projected = projected + proj_recv[i, k].astype(jnp.float32)
                summed = summed + sums_recv[i, k]

        with jax.named_scope("E_attn"):
            inv_rms = lax.rsqrt(jnp.sum(summed, axis=1, keepdims=True) / (feat * m) + epsilon)
            projected = projected * inv_rms
            queries = jnp.concatenate(
                [
                    projected[:, h * HD : (h + 1) * HD].reshape(part_requests, 1, BRANCH, HD)
                    for h in range(heads)
                ],
                axis=1,
            ).reshape(own * heads, HD).astype(jnp.bfloat16)
            now = pl.ds(pl.multiple_of(e * own, own), own)
            tree_keys[b, now] = projected[:, head_cols : head_cols + HD].astype(jnp.bfloat16)
            tree_values[b, now] = projected[:, head_cols + HD :].astype(jnp.bfloat16)

            @pl.when(i == 0)
            def _():
                loads[3].wait()

            tall = heads * BRANCH
            tree_scores = dot32_t(queries, tree_keys[b]) * HD ** (-0.5)
            allowed = jnp.broadcast_to(
                mask_now.reshape(part_requests, 1, BRANCH, DEPTHS * own),
                (part_requests, heads, BRANCH, DEPTHS * own),
            ).reshape(own * heads, DEPTHS * own)
            tree_scores = jnp.where(allowed > 0.5, tree_scores, masked_score)
            cache_scores = []
            position = lax.broadcasted_iota(jnp.int32, (tall, CACHE), 1)
            for r in range(part_requests):
                request = b * part_requests + r
                scores = dot32_t(queries[r * tall : (r + 1) * tall], cache[request, 0])
                scores = scores * HD ** (-0.5)
                cache_scores.append(jnp.where(position < len_ref[request], scores, masked_score))
            cache_scores = jnp.concatenate(cache_scores, axis=0)
            row_max = jnp.maximum(
                jnp.max(cache_scores, axis=1, keepdims=True),
                jnp.max(tree_scores, axis=1, keepdims=True),
            )
            cache_exp = jnp.exp(cache_scores - row_max)
            tree_exp = jnp.exp(tree_scores - row_max)
            denominator = jnp.sum(cache_exp, axis=1, keepdims=True) + jnp.sum(
                tree_exp, axis=1, keepdims=True
            )
            cache_weights = (cache_exp / denominator).astype(jnp.bfloat16)
            tree_weights = (tree_exp / denominator).astype(jnp.bfloat16)
            mixed = jnp.concatenate(
                [
                    dot32(cache_weights[r * tall : (r + 1) * tall], cache[b * part_requests + r, 1])
                    for r in range(part_requests)
                ],
                axis=0,
            ) + dot32(tree_weights, tree_values[b])
            mixed = mixed.reshape(part_requests, heads, BRANCH, HD)
            for h in range(heads):
                att[i, d, :, h * HD : (h + 1) * HD] = (
                    mixed[:, h].reshape(own, HD).astype(jnp.bfloat16)
                )
            for k in range(m - 1):
                att_copy(i, k).start()

        with jax.named_scope("F_mid"):
            run(i, 2)

        with jax.named_scope("G_attwait"):
            for k in range(m - 1):
                att_copy(i, k).wait_recv()

            @pl.when(i == 0)
            def _():
                for load in loads[4:]:
                    load.wait()

        with jax.named_scope("H_out"):
            attended = att[i].reshape(rows, head_cols)
            last = i >= tail
            for q in range(n):
                seg = jnp.where(last & (t == 0), n - 1 - q, q)
                block = dot32(attended, wo[seg])
                for j in range(per):
                    part[b, seg * per + j] = block[:, j * width : (j + 1) * width]

                @pl.when((t == 0) & (q * per < right_limit(i)))
                def _():
                    for j in range(per):
                        c = seg * per + jnp.where(last, per - 1 - j, j)
                        right_send[i, c] = part[b, c].astype(jnp.bfloat16)
                        right_copy(i, c).start()

                @pl.when((t == n - 1) & (q * per < left_limit(i)))
                def _():
                    for j in range(per):
                        c = seg * per + j
                        left_send[i, c] = part[b, c].astype(jnp.bfloat16)
                        left_copy(i, c).start()

        return carry

    lax.fori_loop(0, steps, step, 0)
    with jax.named_scope("Z_tail"):
        for p in range(tail, steps):
            relay_rest(p)
            finish_last(p)

    def drain(i, carry):
        for k in range(m - 1):
            proj_copy(i, k).wait_send()
            dsum_copy(i, k).wait_send()
            att_copy(i, k).wait_send()
        for s in range(chunks):

            @pl.when((t < n - 1) & (s < right_limit(i)))
            def _():
                right_copy(i, right_chunk(i, s)).wait_send()

            @pl.when((t > 0) & (s < left_limit(i)))
            def _():
                left_copy(i, s).wait_send()

        return carry

    with jax.named_scope("Z_drain"):
        lax.fori_loop(0, steps, drain, 0)


def kernel_shards(
    root_features,
    branch_embeds,
    parents,
    cache_lengths,
    cache_kv,
    norm_gain,
    w_query,
    w_keyval,
    w_out,
):
    n = lax.axis_size("tensor")
    m = lax.axis_size("dp")
    requests, feat = root_features.shape
    own_requests = cache_lengths.shape[0]
    part_requests = own_requests // BATCHES
    own = part_requests * BRANCH
    rows = own * m
    steps = BATCHES * DEPTHS
    head_cols = w_query.shape[1]
    proj_cols = head_cols + 2 * HD
    chunks = n * PER
    width = feat // chunks

    def one_hots(table):
        count = rows
        split = table.reshape(m, BATCHES, part_requests, DEPTHS - 1, BRANCH)
        split = jnp.transpose(split, (3, 1, 0, 2, 4)).reshape((DEPTHS - 1) * BATCHES, count)
        lane = jnp.arange(count, dtype=jnp.int32)
        index = split + (lane // BRANCH * BRANCH)[None, :]
        return (index[:, :, None] == lane[None, None, :]).astype(jnp.bfloat16)

    hot = one_hots(parents)
    bf16, f32 = jnp.bfloat16, jnp.float32
    vmem = pl.BlockSpec(memory_space=pltpu.VMEM)
    smem = pl.BlockSpec(memory_space=pltpu.SMEM)
    hbm = pl.BlockSpec(memory_space=pl.ANY)
    dma = pltpu.SemaphoreType.DMA
    passing = pltpu.VMEM((steps, chunks, rows, width), bf16)
    return pl.pallas_call(
        functools.partial(tree_kernel, n, m),
        out_shape=jax.ShapeDtypeStruct((requests, DEPTHS, BRANCH, feat // n), bf16),
        in_specs=[vmem, hbm, vmem, smem, hbm, vmem, hbm, hbm, hbm],
        out_specs=vmem,
        scratch_shapes=[
            pltpu.VMEM((DEPTHS, requests, BRANCH, feat), bf16),
            pltpu.VMEM(cache_kv.shape, bf16),
            pltpu.VMEM((feat, head_cols), bf16),
            pltpu.VMEM((feat, 2 * HD), bf16),
            pltpu.VMEM((n, head_cols, feat // n), bf16),
            pltpu.VMEM((BATCHES, rows, feat), bf16),
            pltpu.VMEM((BATCHES, chunks, rows, width), f32),
            pltpu.VMEM((BATCHES, chunks, rows, width), f32),
            passing,
            passing,
            passing,
            passing,
            pltpu.VMEM((BATCHES, rows, proj_cols), f32),
            pltpu.VMEM((steps, m, own, proj_cols), bf16),
            pltpu.VMEM((steps, m - 1, own, proj_cols), bf16),
            pltpu.VMEM((steps, m, own, HD), f32),
            pltpu.VMEM((steps, m - 1, own, HD), f32),
            pltpu.VMEM((BATCHES, DEPTHS * own, HD), bf16),
            pltpu.VMEM((BATCHES, DEPTHS * own, HD), bf16),
            pltpu.VMEM((BATCHES, rows, DEPTHS * own), bf16),
            pltpu.VMEM((steps, m, own, head_cols), bf16),
            dma((3 + n + DEPTHS,)),
            dma((steps, chunks)),
            dma((steps, chunks)),
            dma((steps, chunks)),
            dma((steps, chunks)),
            dma((steps, m - 1)),
            dma((steps, m - 1)),
            dma((steps, m - 1)),
            dma((steps, m - 1)),
            dma((steps, m - 1)),
            dma((steps, m - 1)),
        ],
        compiler_params=pltpu.CompilerParams(
            collective_id=0, has_side_effects=True, vmem_limit_bytes=60 * 1024 * 1024
        ),
    )(
        root_features,
        branch_embeds,
        hot,
        cache_lengths,
        cache_kv,
        norm_gain[None, :],
        w_query,
        w_keyval.reshape(feat, 2 * HD),
        w_out,
    )


def solution(mesh):
    in_line = 1 < mesh.shape["tensor"] <= 8 and mesh.shape["dp"] > 1
    return jax.shard_map(
        kernel_shards if in_line else shards,
        mesh=mesh,
        in_specs=(
            P("groups", "dp"),
            P("groups", None, None, "dp"),
            P("groups", None, None),
            P(("groups", "dp")),
            P(("groups", "dp"), None, None, "tensor"),
            P("dp"),
            P("dp", "tensor"),
            P("dp", None, "tensor"),
            P("tensor", "dp"),
        ),
        out_specs=P("groups", None, None, ("dp", "tensor")),
        check_vma=False,
    )
```

```python
import functools

import jax
import jax.numpy as jnp
from jax import lax
from jax.experimental import pallas as pl
from jax.experimental.pallas import tpu as pltpu
from jax.sharding import PartitionSpec as P

D = 16384
HD = 128
BRANCH = 8
DEPTHS = 4
CACHE = 512
BATCHES = 2
PER = 4
HOP = 2.8
PACE = 0.65
PERIOD = 12.5
TURN = 7.2
PROJ_TRIP = 2.9
SLACK = 0.5
HOLD = 1.25


epsilon = 1e-05
masked_score = -1e30


def ancestor_path(parent_table, tree_level):
    current = jnp.broadcast_to(
        jnp.arange(BRANCH, dtype=jnp.int32)[None, :], (parent_table.shape[0], BRANCH)
    )
    path_nodes = [current]
    for upper in range(tree_level, 0, -1):
        current = jnp.take_along_axis(parent_table[:, upper - 1], current, axis=1)
        path_nodes.append(current)
    return path_nodes[::-1]


def tree_mask_of(parent_table, tree_level):
    path_nodes = ancestor_path(parent_table, tree_level)
    columns = jnp.arange(BRANCH, dtype=jnp.int32)
    blocks = []
    for other_level in range(DEPTHS):
        if other_level <= tree_level:
            blocks.append(columns[None, None, :] == path_nodes[other_level][:, :, None])
        else:
            blocks.append(jnp.zeros((parent_table.shape[0], BRANCH, BRANCH), dtype=bool))
    return jnp.concatenate(blocks, axis=2)


def shards(
    root_features,
    branch_embeds,
    parents,
    cache_lengths,
    cache_kv,
    norm_gain,
    w_query,
    w_keyval,
    w_out,
):
    request_count, feat_cols = root_features.shape
    local_requests = cache_lengths.shape[0]
    head_cols = w_query.shape[1]
    kv_cols = w_keyval.shape[2]
    kv_local = kv_cols // HD
    all_rows = request_count * BRANCH
    own_rows = local_requests * BRANCH
    share_cols = feat_cols // lax.axis_size("tensor")
    dp_index = lax.axis_index("dp")
    tensor_index = lax.axis_index("tensor")
    weights = jnp.concatenate([w_query, w_keyval.reshape(feat_cols, 2 * kv_cols)], axis=1)
    gain = norm_gain.astype(jnp.float32)
    own_parents = lax.dynamic_slice_in_dim(parents, dp_index * local_requests, local_requests, 0)
    cache_keys = cache_kv[:, 0].reshape(local_requests, CACHE, kv_local, HD)
    cache_values = cache_kv[:, 1].reshape(local_requests, CACHE, kv_local, HD)
    positions = jnp.arange(CACHE, dtype=jnp.int32)
    cache_valid = positions[None, :] < cache_lengths[:, None]
    tree_keys = jnp.zeros((local_requests, DEPTHS * BRANCH, kv_local, HD), jnp.bfloat16)
    tree_values = jnp.zeros((local_requests, DEPTHS * BRANCH, kv_local, HD), jnp.bfloat16)
    results = []
    previous = None
    for tree_level in range(DEPTHS):
        if tree_level == 0:
            parent = jnp.broadcast_to(root_features[:, None, :], (request_count, BRANCH, feat_cols))
        else:
            parent = jnp.take_along_axis(previous, parents[:, tree_level - 1][:, :, None], axis=1)
        node_state = parent.astype(jnp.float32) + branch_embeds[:, tree_level].astype(jnp.float32)
        flat_state = node_state.reshape(all_rows, feat_cols)
        square_sums = jnp.sum(flat_state * flat_state, axis=1)
        scaled = (flat_state * gain).astype(jnp.bfloat16)
        total_sums = lax.psum(square_sums, "dp")
        own_sums = lax.dynamic_slice_in_dim(total_sums, dp_index * own_rows, own_rows, 0)
        proj_terms = lax.psum_scatter(
            jnp.dot(scaled, weights, preferred_element_type=jnp.float32).astype(jnp.bfloat16),
            "dp",
            scatter_dimension=0,
            tiled=True,
        ).astype(jnp.float32)
        inv_rms = lax.rsqrt(own_sums / D + epsilon)[:, None]
        projected = (proj_terms * inv_rms).astype(jnp.bfloat16)
        queries = projected[:, :head_cols].reshape(local_requests, BRANCH, kv_local, -1, HD)
        new_keys = projected[:, head_cols : head_cols + kv_cols].reshape(
            local_requests, BRANCH, kv_local, HD
        )
        new_values = projected[:, head_cols + kv_cols :].reshape(
            local_requests, BRANCH, kv_local, HD
        )
        tree_keys = tree_keys.at[:, tree_level * BRANCH : (tree_level + 1) * BRANCH].set(new_keys)
        tree_values = tree_values.at[:, tree_level * BRANCH : (tree_level + 1) * BRANCH].set(
            new_values
        )
        tree_mask = tree_mask_of(own_parents, tree_level)
        cache_scores = jnp.einsum(
            "rbkgd,rckd->rkgbc", queries, cache_keys, preferred_element_type=jnp.float32
        ) * HD ** (-0.5)
        tree_scores = jnp.einsum(
            "rbkgd,rtkd->rkgbt", queries, tree_keys, preferred_element_type=jnp.float32
        ) * HD ** (-0.5)
        cache_scores = jnp.where(cache_valid[:, None, None, None, :], cache_scores, masked_score)
        tree_scores = jnp.where(tree_mask[:, None, None, :, :], tree_scores, masked_score)
        row_max = jnp.maximum(jnp.max(cache_scores, axis=4), jnp.max(tree_scores, axis=4))[
            ..., None
        ]
        cache_exp = jnp.exp(cache_scores - row_max)
        tree_exp = jnp.exp(tree_scores - row_max)
        denominator = jnp.sum(cache_exp, axis=4, keepdims=True) + jnp.sum(
            tree_exp, axis=4, keepdims=True
        )
        cache_weights = (cache_exp / denominator).astype(jnp.bfloat16)
        tree_weights = (tree_exp / denominator).astype(jnp.bfloat16)
        mixed = jnp.einsum(
            "rkgbc,rckd->rbkgd", cache_weights, cache_values, preferred_element_type=jnp.float32
        )
        mixed = mixed + jnp.einsum(
            "rkgbt,rtkd->rbkgd", tree_weights, tree_values, preferred_element_type=jnp.float32
        )
        attended = mixed.reshape(own_rows, head_cols).astype(jnp.bfloat16)
        partial_out = jnp.dot(
            lax.all_gather(attended, "dp", axis=0, tiled=True),
            w_out,
            preferred_element_type=jnp.float32,
        )
        share_sums = lax.psum_scatter(
            partial_out.astype(jnp.bfloat16), "tensor", scatter_dimension=1, tiled=True
        ).astype(jnp.float32)
        residual = lax.dynamic_slice_in_dim(flat_state, tensor_index * share_cols, share_cols, 1)
        fresh_share = (residual + share_sums).astype(jnp.bfloat16)
        if tree_level + 1 < DEPTHS:
            gathered = lax.all_gather(fresh_share, "tensor", axis=1, tiled=True)
            previous = gathered.reshape(request_count, BRANCH, feat_cols)
        results.append(fresh_share.reshape(request_count, BRANCH, share_cols))
    return jnp.stack(results, axis=1)


MESH = pl.DeviceIdType.MESH


def dot32(a, b):
    return jnp.dot(a, b, preferred_element_type=jnp.float32)


def dot32_t(a, b):
    return lax.dot_general(a, b, (((1,), (1,)), ((), ())), preferred_element_type=jnp.float32)


def timetable(n, chunks):
    per = chunks // n
    jobs = []
    for s in range(chunks):
        for hops in range(1, n - 1):
            jobs.append((HOP * hops + PACE * s, hops, s))
        if s % per == per - 1:
            jobs.append((HOP * (n - 1) + PACE * s + SLACK, n - 1, s // per))
    phases = [[] for _ in range(3 + n)]
    for when, hops, s in jobs:
        age = 1
        while when >= PERIOD:
            age, when = age + 1, when - PERIOD
        phase = 0 if when < PERIOD - TURN else 1 if when < PERIOD - TURN + PROJ_TRIP else 2
        if age > BATCHES or (age == BATCHES and phase > 0):
            age, phase, when = BATCHES, 0, when + PERIOD * (age - BATCHES)
        elif when < HOLD and age > 1 and hops < n - 1:
            age, phase = age - 1, 3 + int(when * n / HOLD)
        phases[phase].append((when, -age, hops, s))
    return [[(-age, hops, s) for _, age, hops, s in sorted(phase)] for phase in phases]


def tree_kernel(
    n,
    m,
    root_ref,
    emb_hbm,
    parents_ref,
    len_ref,
    cache_hbm,
    gain_ref,
    wq_hbm,
    wkv_hbm,
    wo_hbm,
    out_ref,
    hot,
    gain,
    emb,
    cache,
    wq,
    pairs,
    apart,
    wkv,
    wo,
    scaled,
    state,
    part,
    right_send,
    right_recv,
    left_send,
    left_recv,
    proj,
    proj_send,
    proj_recv,
    squares,
    sums_recv,
    tree_keys,
    tree_values,
    tree_mask,
    att,
    load_sem,
    right_ssem,
    right_rsem,
    left_ssem,
    left_rsem,
    proj_ssem,
    proj_rsem,
    dsum_ssem,
    dsum_rsem,
    att_ssem,
    att_rsem,
):
    t = lax.axis_index("tensor")
    d = lax.axis_index("dp")
    requests, feat = root_ref.shape
    own_requests = requests // m
    part_requests = own_requests // BATCHES
    own = part_requests * BRANCH
    rows = own * m
    head_cols = wq.shape[1]
    heads = head_cols // HD
    steps = BATCHES * DEPTHS
    chunks, _, width = right_send.shape[1:]
    per = chunks // n
    tail = steps - BATCHES

    def cols_of(c, count=1):
        return slice(c * width, (c + count) * width)

    def batch_rows(b):
        return [pl.ds(k * own_requests + b * part_requests, part_requests) for k in range(m)]

    def joined(blocks, columns):
        return jnp.concatenate(blocks, axis=0).astype(jnp.float32).reshape(rows, columns)

    loads = [
        pltpu.make_async_copy(emb_hbm.at[:, 0], emb.at[0], load_sem.at[0]),
        pltpu.make_async_copy(wkv_hbm, pairs, load_sem.at[2]),
        pltpu.make_async_copy(wq_hbm, wq, load_sem.at[1]),
        pltpu.make_async_copy(cache_hbm, cache, load_sem.at[3]),
    ]
    for s in range(n):
        columns = slice(s * per * width, (s + 1) * per * width)
        loads.append(pltpu.make_async_copy(wo_hbm.at[:, columns], wo.at[s], load_sem.at[4 + s]))
    for e in range(1, DEPTHS):
        loads.append(
            pltpu.make_async_copy(emb_hbm.at[:, e], emb.at[e], load_sem.at[3 + n + e])
        )
    for load in loads:
        load.start()

    dp_to = [lax.rem(d + k, m) for k in range(1, m)]

    barrier = pltpu.get_barrier_semaphore()
    for peer in dp_to:
        pl.semaphore_signal(barrier, inc=1, device_id={"dp": peer}, device_id_type=MESH)

    for k in range(1, n):
        peer = lax.rem(t + k, n)
        pl.semaphore_signal(barrier, inc=1, device_id={"tensor": peer}, device_id_type=MESH)

    def right_copy(p, c):
        return pltpu.make_async_remote_copy(
            src_ref=right_send.at[p, c],
            dst_ref=right_recv.at[p, c],
            send_sem=right_ssem.at[p, c],
            recv_sem=right_rsem.at[p, c],
            device_id={"tensor": lax.rem(t + 1, n)},
            device_id_type=MESH,
        )

    def left_copy(p, c):
        return pltpu.make_async_remote_copy(
            src_ref=left_send.at[p, c],
            dst_ref=left_recv.at[p, c],
            send_sem=left_ssem.at[p, c],
            recv_sem=left_rsem.at[p, c],
            device_id={"tensor": lax.rem(t + n - 1, n)},
            device_id_type=MESH,
        )

    def proj_copy(i, k):
        return pltpu.make_async_remote_copy(
            src_ref=proj_send.at[i, dp_to[k]],
            dst_ref=proj_recv.at[i, k],
            send_sem=proj_ssem.at[i, k],
            recv_sem=proj_rsem.at[i, k],
            device_id={"dp": dp_to[k]},
            device_id_type=MESH,
        )

    def dsum_copy(i, k):
        return pltpu.make_async_remote_copy(
            src_ref=squares.at[i, dp_to[k]],
            dst_ref=sums_recv.at[i, k],
            send_sem=dsum_ssem.at[i, k],
            recv_sem=dsum_rsem.at[i, k],
            device_id={"dp": dp_to[k]},
            device_id_type=MESH,
        )

    def att_copy(i, k):
        return pltpu.make_async_remote_copy(
            src_ref=att.at[i, d],
            dst_ref=att.at[i, d],
            send_sem=att_ssem.at[i, k],
            recv_sem=att_rsem.at[i, k],
            device_id={"dp": dp_to[k]},
            device_id_type=MESH,
        )

    def right_limit(p):
        return jnp.where(p < tail, chunks, (n - 1 - t) * per)

    def left_limit(p):
        return jnp.where(p < tail, chunks, t * per)

    def right_chunk(p, s):
        return jnp.where(p < tail, s, chunks - 1 - s)

    def relay_right(p, s):
        @pl.when(s < right_limit(p))
        def _():
            c = right_chunk(p, s)
            right_copy(p, c).wait_recv()
            block = part[lax.rem(p, BATCHES), c] + right_recv[p, c].astype(jnp.float32)
            right_send[p, c] = block.astype(jnp.bfloat16)
            right_copy(p, c).start()

    def relay_left(p, s):
        @pl.when(s < left_limit(p))
        def _():
            left_copy(p, s).wait_recv()
            block = part[lax.rem(p, BATCHES), s] + left_recv[p, s].astype(jnp.float32)
            left_send[p, s] = block.astype(jnp.bfloat16)
            left_copy(p, s).start()

    def relays(p, hops, s):
        for place in range(1, n - 1):
            if hops not in (place, n - 1 - place):
                continue

            @pl.when((t == place) & (p >= 0))
            def _():
                if hops == place:
                    relay_right(p, s)
                if hops == n - 1 - place:
                    relay_left(p, s)

    def product(b, c, count, first):
        block = scaled[b, :, cols_of(c, count)]
        left, right = dot32(block, wq[cols_of(c, count)]), dot32(block, wkv[cols_of(c, count)])
        if first:
            proj[b, :, :head_cols] = left
            proj[b, :, head_cols:] = right
        else:
            proj[b, :, :head_cols] += left
            proj[b, :, head_cols:] += right

    def feed(i, c, node):
        b = lax.rem(i, BATCHES)
        state[b, c] = node
        folded = jnp.zeros((rows, HD), jnp.float32)
        for low in range(0, width, HD):
            piece = node[:, low : low + HD]
            folded = folded + piece * piece
            line = (c * width + low) // HD
            fed = (piece * gain[line : line + 1]).astype(jnp.bfloat16)
            scaled[b, :, line * HD : (line + 1) * HD] = fed
        folded = folded.reshape(m, own, HD)
        if c == 0:
            squares[i] = folded
        else:
            squares[i] += folded

    def keep(e, b, value, local):
        for k, r in enumerate(batch_rows(b)):
            out_ref[r, pl.ds(e, 1), :, local * width : (local + 1) * width] = (
                value[k * own : (k + 1) * own].reshape(part_requests, 1, BRANCH, width)
            )

    def finish(p, seg):
        b = lax.rem(p, BATCHES)
        e = p // BATCHES
        group = range(seg * per, (seg + 1) * per)

        @pl.when(t == 0)
        def _():
            for c in group:
                left_copy(p, c).wait_recv()

        @pl.when(t == n - 1)
        def _():
            for c in group:
                right_copy(p, c).wait_recv()

        whole = [
            (
                state[b, c]
                + part[b, c]
                + right_recv[p, c].astype(jnp.float32)
                + left_recv[p, c].astype(jnp.float32)
            ).astype(jnp.bfloat16)
            for c in group
        ]
        pick = hot[p]
        for c, fresh in zip(group, whole):
            embeds = joined([emb[e + 1, r, :, cols_of(c)] for r in batch_rows(b)], width)
            feed(p + BATCHES, c, dot32(pick, fresh) + embeds)
        product(b, seg * per, per, seg == 0)

        @pl.when(t == seg)
        def _():
            for c, fresh in zip(group, whole):
                keep(e, b, fresh, c % per)

    def finish_last(p):
        b = lax.rem(p, BATCHES)
        e = p // BATCHES
        for local in range(per):
            c = t * per + local

            @pl.when(t > 0)
            def _():
                right_copy(p, c).wait_recv()

            @pl.when(t < n - 1)
            def _():
                left_copy(p, c).wait_recv()

            total = (
                state[b, c]
                + part[b, c]
                + right_recv[p, c].astype(jnp.float32)
                + left_recv[p, c].astype(jnp.float32)
            )
            keep(e, b, total.astype(jnp.bfloat16), local)

    row_id = lax.broadcasted_iota(jnp.int32, (rows, requests), 0)
    request_id = lax.broadcasted_iota(jnp.int32, (rows, requests), 1)

    def first_states(b):
        place = row_id // BRANCH
        request = (
            place // part_requests * own_requests + b * part_requests + place % part_requests
        )
        root_hot = (request == request_id).astype(jnp.bfloat16)
        for c in range(chunks):
            embeds = joined([emb[0, r, :, cols_of(c)] for r in batch_rows(b)], width)
            feed(b, c, dot32(root_hot, root_ref[:, cols_of(c)]) + embeds)

    def first_product(b):
        for c in range(0, chunks, per):
            product(b, c, per, c == 0)

    tree_keys[...] = jnp.zeros_like(tree_keys)
    tree_values[...] = jnp.zeros_like(tree_values)
    tree_mask[...] = jnp.zeros_like(tree_mask)

    @pl.when(t == 0)
    def _():
        right_recv[...] = jnp.zeros_like(right_recv)

    @pl.when(t == n - 1)
    def _():
        left_recv[...] = jnp.zeros_like(left_recv)

    with jax.named_scope("Q_gain"):
        gain[...] = gain_ref[...].astype(jnp.float32)
        if True:
            lane = lax.broadcasted_iota(jnp.int32, (BRANCH, rows), 1)
            for e in range(DEPTHS - 1):
                table = parents_ref[e]
                for b in range(BATCHES):
                    blocks = []
                    for k in range(m):
                        for q in range(part_requests):
                            r = k * own_requests + b * part_requests + q
                            base = (k * part_requests + q) * BRANCH
                            blocks.append(lane == table[:, r : r + 1] + base)
                    stacked = jnp.concatenate([x.astype(jnp.float32) for x in blocks], axis=0)
                    hot[e * BATCHES + b] = stacked.astype(jnp.bfloat16)
    with jax.named_scope("Q_emb"):
        loads[0].wait()
    with jax.named_scope("Q_first"):
        first_states(0)
    with jax.named_scope("Q_kvwait"):
        loads[1].wait()
    with jax.named_scope("Q_apart"):
        block = apart.shape[0]

        def split(j, carry):
            apart[...] = pairs[pl.ds(pl.multiple_of(j * block, block), block)].astype(jnp.float32)
            out = pl.ds(pl.multiple_of(j * (block // 2), block // 2), block // 2)
            wkv[out, :HD] = apart[pl.ds(0, block // 2, stride=2)].astype(jnp.bfloat16)
            wkv[out, HD:] = apart[pl.ds(1, block // 2, stride=2)].astype(jnp.bfloat16)
            return carry

        lax.fori_loop(0, 2 * feat // block, split, 0)
    with jax.named_scope("Q_wqwait"):
        loads[2].wait()
    with jax.named_scope("Q_prod"):
        first_product(0)
    pl.semaphore_wait(barrier, m + n - 2)

    timed = timetable(n, chunks)

    def run(i, phase):
        for age, hops, s in timed[phase]:
            p = i - age
            if hops < n - 1:
                relays(p, hops, s)
            else:

                @pl.when((p >= 0) & (p < tail))
                def _():
                    finish(p, s)

    def relay_rest(p):
        for age in range(max(1, steps - p), BATCHES + 1):
            for phase in range(3 + n):
                for job_age, hops, s in timed[phase]:
                    if job_age == age and hops < n - 1:
                        relays(p, hops, s)

    def step(i, carry):
        b = lax.rem(i, BATCHES)
        e = i // BATCHES

        with jax.named_scope("A_tail"):

            run(i, 0)

        with jax.named_scope("B_send"):
            for k in range(m):
                proj_send[i, k] = proj[b, k * own : (k + 1) * own].astype(jnp.bfloat16)
            for k in range(m - 1):
                proj_copy(i, k).start()
                dsum_copy(i, k).start()

        with jax.named_scope("C_mid"):

            @pl.when(i < BATCHES - 1)
            def _():
                first_states(i + 1)
                first_product(i + 1)

            run(i, 1)
            own_row = lax.broadcasted_iota(jnp.int32, (own, DEPTHS * own), 0)
            own_col = lax.broadcasted_iota(jnp.int32, (own, DEPTHS * own), 1)
            itself = (own_col == own_row + e * own).astype(jnp.float32)
            own_rows = pl.ds(pl.multiple_of(d * own, own), own)
            mask_now = itself + dot32(hot[jnp.maximum(i - BATCHES, 0), own_rows], tree_mask[b])
            tree_mask[b, own_rows] = mask_now.astype(jnp.bfloat16)

        projected = proj[b, pl.ds(pl.multiple_of(d * own, own), own)]
        summed = squares[i, d]
        with jax.named_scope("D_projwait"):
            for k in range(m - 1):
                proj_copy(i, k).wait_recv()
                dsum_copy(i, k).wait_recv()
                projected = projected + proj_recv[i, k].astype(jnp.float32)
                summed = summed + sums_recv[i, k]

        with jax.named_scope("E_attn"):
            inv_rms = lax.rsqrt(jnp.sum(summed, axis=1, keepdims=True) / (feat * m) + epsilon)
            projected = projected * inv_rms
            queries = jnp.concatenate(
                [
                    projected[:, h * HD : (h + 1) * HD].reshape(part_requests, 1, BRANCH, HD)
                    for h in range(heads)
                ],
                axis=1,
            ).reshape(own * heads, HD).astype(jnp.bfloat16)
            now = pl.ds(pl.multiple_of(e * own, own), own)
            tree_keys[b, now] = projected[:, head_cols : head_cols + HD].astype(jnp.bfloat16)
            tree_values[b, now] = projected[:, head_cols + HD :].astype(jnp.bfloat16)

            @pl.when(i == 0)
            def _():
                loads[3].wait()

            tall = heads * BRANCH
            tree_scores = dot32_t(queries, tree_keys[b]) * HD ** (-0.5)
            allowed = jnp.broadcast_to(
                mask_now.reshape(part_requests, 1, BRANCH, DEPTHS * own),
                (part_requests, heads, BRANCH, DEPTHS * own),
            ).reshape(own * heads, DEPTHS * own)
            tree_scores = jnp.where(allowed > 0.5, tree_scores, masked_score)
            cache_scores = []
            position = lax.broadcasted_iota(jnp.int32, (tall, CACHE), 1)
            for r in range(part_requests):
                request = b * part_requests + r
                scores = dot32_t(queries[r * tall : (r + 1) * tall], cache[request, 0])
                scores = scores * HD ** (-0.5)
                cache_scores.append(jnp.where(position < len_ref[request], scores, masked_score))
            cache_scores = jnp.concatenate(cache_scores, axis=0)
            row_max = jnp.maximum(
                jnp.max(cache_scores, axis=1, keepdims=True),
                jnp.max(tree_scores, axis=1, keepdims=True),
            )
            cache_exp = jnp.exp(cache_scores - row_max)
            tree_exp = jnp.exp(tree_scores - row_max)
            denominator = jnp.sum(cache_exp, axis=1, keepdims=True) + jnp.sum(
                tree_exp, axis=1, keepdims=True
            )
            cache_weights = (cache_exp / denominator).astype(jnp.bfloat16)
            tree_weights = (tree_exp / denominator).astype(jnp.bfloat16)
            mixed = jnp.concatenate(
                [
                    dot32(cache_weights[r * tall : (r + 1) * tall], cache[b * part_requests + r, 1])
                    for r in range(part_requests)
                ],
                axis=0,
            ) + dot32(tree_weights, tree_values[b])
            mixed = mixed.reshape(part_requests, heads, BRANCH, HD)
            for h in range(heads):
                att[i, d, :, h * HD : (h + 1) * HD] = (
                    mixed[:, h].reshape(own, HD).astype(jnp.bfloat16)
                )
            for k in range(m - 1):
                att_copy(i, k).start()

        with jax.named_scope("F_mid"):
            run(i, 2)

        with jax.named_scope("G_attwait"):
            for k in range(m - 1):
                att_copy(i, k).wait_recv()

            @pl.when(i == 0)
            def _():
                for load in loads[4:]:
                    load.wait()

        with jax.named_scope("H_out"):
            attended = att[i].reshape(rows, head_cols)
            last = i >= tail
            for q in range(n):
                if q > 0:
                    run(i, 2 + q)
                seg = jnp.where(last & (t == 0), n - 1 - q, q)
                block = dot32(attended, wo[seg])
                for j in range(per):
                    part[b, seg * per + j] = block[:, j * width : (j + 1) * width]

                @pl.when((t == 0) & (q * per < right_limit(i)))
                def _():
                    for j in range(per):
                        c = seg * per + jnp.where(last, per - 1 - j, j)
                        right_send[i, c] = part[b, c].astype(jnp.bfloat16)
                        right_copy(i, c).start()

                @pl.when((t == n - 1) & (q * per < left_limit(i)))
                def _():
                    for j in range(per):
                        c = seg * per + j
                        left_send[i, c] = part[b, c].astype(jnp.bfloat16)
                        left_copy(i, c).start()

            run(i, 2 + n)
        return carry

    def drain(i, carry):
        for k in range(m - 1):
            proj_copy(i, k).wait_send()
            dsum_copy(i, k).wait_send()
            att_copy(i, k).wait_send()
        for s in range(chunks):

            @pl.when((t < n - 1) & (s < right_limit(i)))
            def _():
                right_copy(i, right_chunk(i, s)).wait_send()

            @pl.when((t > 0) & (s < left_limit(i)))
            def _():
                left_copy(i, s).wait_send()

        return carry

    lax.fori_loop(0, steps, step, 0)
    with jax.named_scope("Z_tail"):
        for p in range(tail, steps - 1):
            relay_rest(p)
            finish_last(p)
        relay_rest(steps - 1)
        lax.fori_loop(0, steps - 1, drain, 0)
        finish_last(steps - 1)
        drain(steps - 1, 0)


def kernel_shards(
    root_features,
    branch_embeds,
    parents,
    cache_lengths,
    cache_kv,
    norm_gain,
    w_query,
    w_keyval,
    w_out,
):
    n = lax.axis_size("tensor")
    m = lax.axis_size("dp")
    requests, feat = root_features.shape
    own_requests = cache_lengths.shape[0]
    part_requests = own_requests // BATCHES
    own = part_requests * BRANCH
    rows = own * m
    steps = BATCHES * DEPTHS
    head_cols = w_query.shape[1]
    proj_cols = head_cols + 2 * HD
    chunks = n * PER
    width = feat // chunks

    bf16, f32 = jnp.bfloat16, jnp.float32
    vmem = pl.BlockSpec(memory_space=pltpu.VMEM)
    smem = pl.BlockSpec(memory_space=pltpu.SMEM)
    hbm = pl.BlockSpec(memory_space=pl.ANY)
    dma = pltpu.SemaphoreType.DMA
    passing = pltpu.VMEM((steps, chunks, rows, width), bf16)
    return pl.pallas_call(
        functools.partial(tree_kernel, n, m),
        out_shape=jax.ShapeDtypeStruct((requests, DEPTHS, BRANCH, feat // n), bf16),
        in_specs=[vmem, hbm, vmem, smem, hbm, vmem, hbm, hbm, hbm],
        out_specs=vmem,
        scratch_shapes=[
            pltpu.VMEM(((DEPTHS - 1) * BATCHES, rows, rows), bf16),
            pltpu.VMEM((feat // HD, HD), f32),
            pltpu.VMEM((DEPTHS, requests, BRANCH, feat), bf16),
            pltpu.VMEM(cache_kv.shape, bf16),
            pltpu.VMEM((feat, head_cols), bf16),
            pltpu.VMEM((2 * feat, HD), bf16),
            pltpu.VMEM((1024, HD), f32),
            pltpu.VMEM((feat, 2 * HD), bf16),
            pltpu.VMEM((n, head_cols, feat // n), bf16),
            pltpu.VMEM((BATCHES, rows, feat), bf16),
            pltpu.VMEM((BATCHES, chunks, rows, width), f32),
            pltpu.VMEM((BATCHES, chunks, rows, width), f32),
            passing,
            passing,
            passing,
            passing,
            pltpu.VMEM((BATCHES, rows, proj_cols), f32),
            pltpu.VMEM((steps, m, own, proj_cols), bf16),
            pltpu.VMEM((steps, m - 1, own, proj_cols), bf16),
            pltpu.VMEM((steps, m, own, HD), f32),
            pltpu.VMEM((steps, m - 1, own, HD), f32),
            pltpu.VMEM((BATCHES, DEPTHS * own, HD), bf16),
            pltpu.VMEM((BATCHES, DEPTHS * own, HD), bf16),
            pltpu.VMEM((BATCHES, rows, DEPTHS * own), bf16),
            pltpu.VMEM((steps, m, own, head_cols), bf16),
            dma((3 + n + DEPTHS,)),
            dma((steps, chunks)),
            dma((steps, chunks)),
            dma((steps, chunks)),
            dma((steps, chunks)),
            dma((steps, m - 1)),
            dma((steps, m - 1)),
            dma((steps, m - 1)),
            dma((steps, m - 1)),
            dma((steps, m - 1)),
            dma((steps, m - 1)),
        ],
        compiler_params=pltpu.CompilerParams(
            collective_id=0, has_side_effects=True, vmem_limit_bytes=60 * 1024 * 1024
        ),
    )(
        root_features,
        branch_embeds,
        jnp.transpose(parents, (1, 2, 0)),
        cache_lengths,
        cache_kv,
        norm_gain.reshape(feat // HD, HD),
        w_query,
        w_keyval.reshape(2 * feat, HD),
        w_out,
    )


def solution(mesh):
    in_line = 1 < mesh.shape["tensor"] <= 8 and mesh.shape["dp"] > 1
    return jax.shard_map(
        kernel_shards if in_line else shards,
        mesh=mesh,
        in_specs=(
            P("groups", "dp"),
            P("groups", None, None, "dp"),
            P("groups", None, None),
            P(("groups", "dp")),
            P(("groups", "dp"), None, None, "tensor"),
            P("dp"),
            P("dp", "tensor"),
            P("dp", None, "tensor"),
            P("tensor", "dp"),
        ),
        out_specs=P("groups", None, None, ("dp", "tensor")),
        check_vma=False,
    )
```
